128 devices in a mesh: grp: 4 (over x_hi, core), dom: 32 (over z, y, x_lo).
Axes of the slice: x: 4 (x_hi: 2, x_lo: 2; x = x_hi * 2 + x_lo), y: 4, z: 4, core: 2. Of those that a mesh axis runs over, the one named last changes fastest.
Arguments:
- nodes: bfloat16 [131072, 256], P(('grp', 'dom')), may hold values from -8 to 8
- neighbours: int32 [131072, 8], P(('grp', 'dom')), may hold values from 0 to 1279
- send_rows: int32 [32768], P(('grp', 'dom')), may hold values from 0 to 1023
- landmark_ids: int32 [8192], P(('grp', 'dom')), may hold values from 0 to 1023
- w_dst: bfloat16 [256, 256], replicated, may hold values from -0.375 to 0.375
- w_src: bfloat16 [256, 256], replicated, may hold values from -0.375 to 0.375
- w_msg: bfloat16 [256, 256], replicated, may hold values from -0.375 to 0.375
- edge_bias: float32 [256], replicated, may hold values from -4 to 4
- w_query: bfloat16 [256, 256], replicated, may hold values from -0.375 to 0.375
- w_key: bfloat16 [256, 256], replicated, may hold values from -0.375 to 0.375
- w_value: bfloat16 [256, 256], replicated, may hold values from -0.375 to 0.375
- w_out: bfloat16 [256, 256], replicated, may hold values from -0.375 to 0.375
Outputs:
- result: bfloat16 [131072, 256], P(('grp', 'dom'))
- kernel_term: float32 [131072, 256], P(('grp', 'dom'))
The draws below stay inside these ranges and needn't reach their ends.
Inputs may be any that keep to these rules, and one draw needn't show every extreme that they name: `neighbours`: entries index the device's own 1024 rows, then the 128 rows received from the previous partition, then the 128 rows from the next one. `send_rows`: each partition's entries are rows of its own nodes. `landmark_ids`: each partition's entries are rows of its own nodes.
All inputs are finite; a program needn't handle non-finite values.
Results may differ from the reference program's by a relative error of at most 0.0054.
Values may be sent and summed in bfloat16 or wider, within the bound.
A program may use at most 64 MiB of HBM per device.

```python
import math
import jax
import jax.numpy as jnp
from jax import lax

C = 256
M = 8192
NBR = 8
ROWS = 1024
HALO = 128
NODES = 131072
DEVICES = 128


def draw_nodes(key, part):
    base = jax.random.fold_in(key, 17)
    noise_key, direction_key = jax.random.split(base, 2)
    partitions = NODES // ROWS
    noise = jax.random.normal(noise_key, (partitions, ROWS, C), jnp.float32)
    amplitude = 2.0
    direction = jax.random.normal(direction_key, (partitions, 1, C), jnp.float32)
    values = jnp.clip(noise + amplitude * direction, -8.0, 8.0)
    return values.reshape(NODES, C).astype(jnp.bfloat16)


def touch_ends(values, own_key, smallest, largest):
    spot = [jax.random.randint(jax.random.fold_in(own_key, axis), (), 0, length) for axis, length in enumerate(values.shape)]
    main_axis = values.shape.index(max(values.shape))
    neighbour = spot[:main_axis] + [(spot[main_axis] + 1) % values.shape[main_axis]] + spot[main_axis + 1:]
    return values.at[tuple(spot)].set(smallest).at[tuple(neighbour)].set(largest)


def centred(stream_key, dims, deviation, limit, dtype=jnp.bfloat16):
    return jnp.clip(deviation * jax.random.normal(stream_key, dims, jnp.float32), -limit, limit).astype(dtype)


def setup_inputs(seed: int = 0) -> dict:
    streams_of = jax.random.split(jax.random.key(seed), 13)
    return {
        "nodes": draw_nodes(jax.random.fold_in(streams_of[12], 71), 0),
        "neighbours": touch_ends(jax.random.randint(streams_of[1], (NODES, NBR), 0, ROWS + 2 * HALO), jax.random.fold_in(streams_of[1], 1), 0, (ROWS + 2 * HALO) - 1).astype(jnp.int32),
        "send_rows": touch_ends(jax.random.randint(streams_of[2], (2 * HALO * DEVICES,), 0, ROWS), jax.random.fold_in(streams_of[2], 1), 0, ROWS - 1).astype(jnp.int32),
        "landmark_ids": touch_ends(jax.random.randint(streams_of[3], (M,), 0, ROWS), jax.random.fold_in(streams_of[3], 1), 0, ROWS - 1).astype(jnp.int32),
        "w_dst": centred(streams_of[4], (C, C), C ** -0.5, 0.375),
        "w_src": centred(streams_of[5], (C, C), C ** -0.5, 0.375),
        "w_msg": centred(streams_of[6], (C, C), C ** -0.5, 0.375),
        "edge_bias": centred(streams_of[7], (C,), 1.0, 4.0, jnp.float32),
        "w_query": centred(streams_of[8], (C, C), C ** -0.5, 0.375),
        "w_key": centred(streams_of[9], (C, C), C ** -0.5, 0.375),
        "w_value": centred(streams_of[10], (C, C), C ** -0.5, 0.375),
        "w_out": centred(streams_of[11], (C, C), C ** -0.5, 0.375),
    }


def rms_scale(values):
    return values * lax.rsqrt(lax.optimization_barrier(jnp.mean(values * values, axis=-1, keepdims=True)) + 1e-06)

def reference(nodes, neighbours, send_rows, landmark_ids, w_dst, w_src, w_msg, edge_bias, w_query, w_key, w_value, w_out):
    parts = nodes.reshape(DEVICES, ROWS, C)
    sends = send_rows.reshape(DEVICES, 2 * HALO)
    outgoing = jax.vmap(lambda block, picks: block[picks])(parts, sends)
    from_prev = jnp.roll(outgoing[:, HALO:], 1, axis=0)
    from_next = jnp.roll(outgoing[:, :HALO], -1, axis=0)
    extended = jnp.concatenate([parts, from_prev, from_next], axis=1)
    links = neighbours.reshape(DEVICES, ROWS, NBR)

    def edge_layer(inputs):
        block, table, slots = inputs
        source = jnp.dot(table, w_src, preferred_element_type=jnp.float32)
        target = jnp.dot(block, w_dst, preferred_element_type=jnp.float32)
        preact = target[:, None, :] + source[slots] + edge_bias
        messages = lax.optimization_barrier(jnp.mean(jax.nn.gelu(preact), axis=1)).astype(jnp.bfloat16)
        return (block.astype(jnp.float32) + jnp.dot(messages, w_msg, preferred_element_type=jnp.float32)).astype(jnp.bfloat16)
    updated = lax.map(edge_layer, (parts, extended, links))
    normed = rms_scale(updated.astype(jnp.float32)).astype(jnp.bfloat16)
    flat = normed.reshape(NODES, C)
    query = jnp.dot(flat, w_query, preferred_element_type=jnp.float32).astype(jnp.bfloat16)
    value = jnp.dot(flat, w_value, preferred_element_type=jnp.float32).astype(jnp.bfloat16)
    chosen = jax.vmap(lambda block, picks: block[picks])(normed, landmark_ids.reshape(DEVICES, M // DEVICES)).reshape(M, C)
    keys = jnp.dot(chosen, w_key, preferred_element_type=jnp.float32).astype(jnp.bfloat16)
    scale = 2.0 * C ** (-0.5)
    block_size = math.gcd(M, 256)

    def landmark_block(key_rows):
        kernel = jnp.exp(jnp.dot(query, key_rows.T, preferred_element_type=jnp.float32) * scale).astype(jnp.bfloat16)
        return lax.dot_general(kernel, value, (((0,), (0,)), ((), ())), preferred_element_type=jnp.float32)
    sums = lax.map(landmark_block, keys.reshape(M // block_size, block_size, C)).reshape(M, C)
    landmark_sums = sums.astype(jnp.bfloat16)

    def node_block(query_rows):
        kernel = jnp.exp(jnp.dot(query_rows, keys.T, preferred_element_type=jnp.float32) * scale).astype(jnp.bfloat16)
        smooth = jnp.dot(kernel, landmark_sums, preferred_element_type=jnp.float32)
        return rms_scale(smooth)
    kernel_term = lax.map(node_block, query.reshape(DEVICES, ROWS, C)).reshape(NODES, C)
    scaled = kernel_term.astype(jnp.bfloat16)
    result = updated.reshape(NODES, C).astype(jnp.float32) + jnp.dot(scaled, w_out, preferred_element_type=jnp.float32)
    return (result.astype(jnp.bfloat16), kernel_term)
```

```python
import functools
import math

import jax
import jax.numpy as jnp
from jax import lax
from jax.experimental import pallas as pl
from jax.experimental.pallas import tpu as pltpu
from jax.sharding import PartitionSpec as P

bf16 = jnp.bfloat16
f32 = jnp.float32
MESH = pl.DeviceIdType.MESH
AXES = ("grp", "dom")
VM = pl.BlockSpec(memory_space=pltpu.VMEM)


def dotf(a, b):
    return jnp.dot(a, b, preferred_element_type=f32)


def dot_nt(a, b):
    return lax.dot_general(a, b, (((1,), (1,)), ((), ())), preferred_element_type=f32)


def dot_tn(a, b):
    return lax.dot_general(a, b, (((0,), (0,)), ((), ())), preferred_element_type=f32)


def rows_at(start, size):
    return pl.ds(pl.multiple_of(start, size), size)


def gelu(x):
    return 0.5 * x * (1.0 + jnp.tanh(math.sqrt(2.0 / math.pi) * (x + 0.044715 * (x * x * x))))


def pick_rows(ids, table):
    rows = table.shape[0]
    count = ids.shape[1]
    chosen = lax.broadcasted_iota(jnp.int32, (rows, count), 0) == ids
    return dot_tn(chosen.astype(f32).astype(bf16), table).astype(bf16)


def enter(partners):
    barrier = pltpu.get_barrier_semaphore()
    for device in partners:
        pl.semaphore_signal(barrier, inc=1, device_id=device, device_id_type=MESH)
    pl.semaphore_wait(barrier, len(partners))


def halo_kernel(groups, doms, nodes, send_rows, halo, outgoing, landing, send_sem, recv_sem):
    count = groups * doms
    me = lax.axis_index("grp") * doms + lax.axis_index("dom")
    before = (me + count - 1) % count
    after = (me + 1) % count
    prev = (before // doms, before % doms)
    nxt = (after // doms, after % doms)
    half = halo.shape[0] // 2
    outgoing[...] = pick_rows(send_rows[...], nodes[...])
    enter((prev, nxt))
    to_prev = pltpu.make_async_remote_copy(
        src_ref=outgoing.at[:half],
        dst_ref=landing.at[half:],
        send_sem=send_sem.at[0],
        recv_sem=recv_sem.at[0],
        device_id=prev,
        device_id_type=MESH,
    )
    to_next = pltpu.make_async_remote_copy(
        src_ref=outgoing.at[half:],
        dst_ref=landing.at[:half],
        send_sem=send_sem.at[1],
        recv_sem=recv_sem.at[1],
        device_id=nxt,
        device_id_type=MESH,
    )
    to_prev.start()
    to_next.start()
    to_prev.wait()
    to_next.wait()
    halo[...] = landing[...]


def halo_rows(groups, doms, nodes, send_rows):
    count = send_rows.shape[0]
    shape = (count, nodes.shape[1])
    return pl.pallas_call(
        functools.partial(halo_kernel, groups, doms),
        out_shape=jax.ShapeDtypeStruct(shape, bf16),
        in_specs=[VM, VM],
        out_specs=VM,
        scratch_shapes=[
            pltpu.VMEM(shape, bf16),
            pltpu.VMEM(shape, bf16),
            pltpu.SemaphoreType.DMA((2,)),
            pltpu.SemaphoreType.DMA((2,)),
        ],
        compiler_params=pltpu.CompilerParams(collective_id=0, has_side_effects=True),
        name="halo",
    )(nodes, send_rows.reshape(1, count))


def front_kernel(
    nodes, halo, nbr, ids, w_dst, w_src, w_msg, bias, w_query, w_key, w_value,
    updated, query, value, keys, source, target, onehot, messages, normed,
):
    rows, channels = nodes.shape
    total = source.shape[0]
    slots = nbr.shape[1]
    block = onehot.shape[0] // slots
    source[:rows, :] = dotf(nodes[...], w_src[...]).astype(bf16)
    source[rows:, :] = dotf(halo[...], w_src[...]).astype(bf16)
    target[...] = dotf(nodes[...], w_dst[...]) + bias[...]

    def body(step, carry):
        here = rows_at(step * block, block)
        index = nbr[here, :]
        lane = lax.broadcasted_iota(jnp.int32, (block, total), 1).astype(jnp.int16)
        for k in range(slots):
            column = jnp.broadcast_to(index[:, k : k + 1], (block, total)).astype(jnp.int16)
            onehot[k * block : (k + 1) * block, :] = jnp.where(
                column == lane, jnp.ones((), bf16), jnp.zeros((), bf16)
            )
        picked = dotf(onehot[...], source[...])
        base = target[here, :]
        total_gelu = jnp.zeros((block, channels), f32)
        for k in range(slots):
            total_gelu = total_gelu + gelu(picked[k * block : (k + 1) * block] + base)
        messages[here, :] = (total_gelu * (1.0 / slots)).astype(bf16)
        return carry

    lax.fori_loop(0, rows // block, body, 0)
    new = (nodes[...].astype(f32) + dotf(messages[...], w_msg[...])).astype(bf16)
    updated[...] = new
    wide = new.astype(f32)
    unit = (wide * lax.rsqrt(jnp.mean(wide * wide, axis=-1, keepdims=True) + 1e-6)).astype(bf16)
    normed[...] = unit
    query[...] = dotf(unit, w_query[...]).astype(bf16)
    value[...] = dotf(unit, w_value[...]).astype(bf16)
    keys[...] = dotf(pick_rows(ids[...], normed[...]), w_key[...]).astype(bf16)


def front(nodes, halo, nbr, ids, w_dst, w_src, w_msg, bias, w_query, w_key, w_value):
    rows, channels = nodes.shape
    total = rows + halo.shape[0]
    count = ids.shape[0]
    slots = nbr.shape[1]
    block = math.gcd(rows, 128)
    full = jax.ShapeDtypeStruct((rows, channels), bf16)
    return pl.pallas_call(
        front_kernel,
        out_shape=(full, full, full, jax.ShapeDtypeStruct((count, channels), bf16)),
        in_specs=[VM] * 11,
        out_specs=(VM,) * 4,
        scratch_shapes=[
            pltpu.VMEM((total, channels), bf16),
            pltpu.VMEM((rows, channels), f32),
            pltpu.VMEM((slots * block, total), bf16),
            pltpu.VMEM((rows, channels), bf16),
            pltpu.VMEM((rows, channels), bf16),
        ],
        compiler_params=pltpu.CompilerParams(vmem_limit_bytes=24 << 20),
        name="front",
    )(
        nodes, halo, nbr, ids.reshape(1, count), w_dst, w_src, w_msg,
        bias.reshape(1, channels), w_query, w_key, w_value,
    )


RING = 4
LOG2E = math.log2(math.e)


def smooth_kernel(
    query, value, keys, smooth,
    all_query, all_value, all_keys, kernel, part, own, sums,
    relay, slabs, mid, low, small, accum, landing, send_sem, recv_sem,
):
    rows, channels = query.shape
    block = keys.shape[0]
    quad, slab = RING * block, RING * RING * block
    half = slab // 2
    chunk = quad

    grp, dom = lax.axis_index("grp"), lax.axis_index("dom")
    core, x = grp % 2, (grp // 2) * 2 + dom % 2
    y, z = (dom // 2) % RING, dom // (2 * RING)
    inner = y * (1 - core) + z * core
    outer = z * (1 - core) + y * core

    def device(i, m, o, c):
        yy = i * (1 - core) + o * core
        zz = o * (1 - core) + i * core
        return ((m // 2) * 2 + c, zz * (2 * RING) + yy * 2 + m % 2)

    def turn(a, d):
        return (a + d) % RING

    inner_peer = {d: device(turn(inner, d), x, outer, core) for d in (1, 2, 3)}
    mid_peer = {d: device(inner, turn(x, d), outer, core) for d in (1, 2, 3)}
    right = device(inner, x, turn(outer, 1), core)
    left = device(inner, x, turn(outer, 3), core)
    other = device(inner, x, outer, 1 - core)
    enter((*inner_peer.values(), *mid_peer.values(), right, left, other))

    used = [0]

    def push(src, dst, where):
        n = used[0]
        used[0] += 1
        copy = pltpu.make_async_remote_copy(
            src_ref=src,
            dst_ref=dst,
            send_sem=send_sem.at[n],
            recv_sem=recv_sem.at[n],
            device_id=where,
            device_id_type=MESH,
        )
        copy.start()
        return copy

    pending = []

    def arrive(copies):
        for copy in copies:
            copy.wait_recv()
            pending.append(copy)

    def slab_at(d):
        return turn(outer, d) * slab

    me_block = (outer * RING * RING + x * RING + inner) * block
    me_quad = (outer * RING + x) * quad

    def gather(first, table, work):
        table[rows_at(me_block, block), :] = first[...]
        arrive([push(first, table.at[rows_at(me_block, block)], inner_peer[d]) for d in (2, 1, 3)])
        here = table.at[rows_at(me_quad, quad)]
        arrive([push(here, here, mid_peer[d]) for d in (2, 1, 3)])
        here = table.at[rows_at(slab_at(0), slab)]
        to_right = push(here, here, right)
        to_left = push(here, here, left)
        work(0)
        arrive([to_right])
        top = table.at[rows_at(slab_at(3), half)]
        far_right = push(top, top, right)
        arrive([to_left])
        bottom = table.at[rows_at(slab_at(1) + half, half)]
        far_left = push(bottom, bottom, left)
        work(3)
        work(1)
        arrive([far_right, far_left])
        work(2)

    all_query[:rows, :] = query[...]
    all_value[:rows, :] = value[...]
    swap_query = push(query, all_query.at[rows:], other)
    swap_value = push(value, all_value.at[rows:], other)

    def kernel_rows(d):
        if d == 0:
            arrive([swap_query])

        def body(step, carry):
            here = rows_at(slab_at(d) + step * chunk, chunk)
            dots = dot_nt(all_keys[here, :], all_query[...])
            kernel[here, :] = jnp.exp2(dots * (2.0 * channels**-0.5 * LOG2E)).astype(bf16)
            return carry

        lax.fori_loop(0, slab // chunk, body, 0)

    gather(keys, all_keys, kernel_rows)
    arrive([swap_value])

    def partial(d, second, extra=None):
        start = slab_at(d) + second * half

        def body(step, carry):
            here = rows_at(start + step * chunk, chunk)
            value_here = dotf(kernel[here, :], all_value[...])
            if extra is not None:
                value_here = value_here + extra[rows_at(step * chunk, chunk), :].astype(f32)
            part[here, :] = value_here.astype(bf16)
            return carry

        lax.fori_loop(0, half // chunk, body, 0)
        return part.at[rows_at(start, half)]

    relay_right = push(partial(2, 0), relay.at[0], right)
    relay_left = push(partial(2, 1), relay.at[1], left)
    right_low = push(partial(1, 1), slabs.at[0, half:], right)
    left_high = push(partial(3, 0), slabs.at[1, :half], left)

    def own_rows(step, carry):
        here = rows_at(slab_at(0) + step * chunk, chunk)
        own[rows_at(step * chunk, chunk), :] = dotf(kernel[here, :], all_value[...])
        return carry

    lax.fori_loop(0, slab // chunk, own_rows, 0)
    arrive([relay_right])
    right_high = push(partial(1, 0, relay.at[0]), slabs.at[0, :half], right)
    arrive([relay_left])
    left_low = push(partial(3, 1, relay.at[1]), slabs.at[1, half:], left)
    arrive([right_low, left_high, right_high, left_low])

    def add_slabs(step, carry):
        here = rows_at(step * chunk, chunk)
        both = slabs[0, here, :].astype(f32) + slabs[1, here, :].astype(f32)
        whole = own[here, :] + both
        own[here, :] = whole
        mid[here, :] = whole.astype(bf16)
        return carry

    lax.fori_loop(0, slab // chunk, add_slabs, 0)
    mid_copies = [
        push(mid.at[rows_at(turn(x, d) * quad, quad)], slabs.at[2, (d - 1) * quad : d * quad], mid_peer[d])
        for d in (2, 1, 3)
    ]
    arrive(mid_copies)
    four = own[rows_at(x * quad, quad), :]
    for d in range(3):
        four = four + slabs[2, d * quad : (d + 1) * quad, :].astype(f32)
    own[:quad, :] = four
    low[...] = four.astype(bf16)
    low_copies = [
        push(low.at[rows_at(turn(inner, d) * block, block)], small.at[d - 1], inner_peer[d])
        for d in (2, 1, 3)
    ]
    arrive(low_copies)
    one = own[rows_at(inner * block, block), :]
    for d in range(3):
        one = one + small[d].astype(f32)
    small[3] = one.astype(bf16)

    tile = rows // 2

    def apply(d):
        def body(step, carry):
            here = rows_at((2 * rows // tile - 1 - step) * tile, tile)
            added = dot_tn(
                kernel[rows_at(slab_at(d), slab), here], sums[rows_at(slab_at(d), slab), :]
            )
            accum[here, :] = added if d == 0 else accum[here, :] + added
            return carry

        if d != 2:
            lax.fori_loop(0, 2 * rows // tile, body, 0)
            return
        lax.fori_loop(0, rows // tile, body, 0)
        swap = push(accum.at[rows:], landing, other)
        lax.fori_loop(rows // tile, 2 * rows // tile, body, 0)
        arrive([swap])

    gather(small.at[3], sums, apply)
    smooth[...] = accum[:rows, :] + landing[...]
    for copy in pending:
        copy.wait_send()


def smooth_rows(query, value, keys):
    rows, channels = query.shape
    block = keys.shape[0]
    marks = RING**3 * block
    slab = RING * RING * block
    copies = 2 * 10 + 2 + 6 + 6 + 1
    return pl.pallas_call(
        smooth_kernel,
        out_shape=jax.ShapeDtypeStruct((rows, channels), f32),
        in_specs=[VM] * 3,
        out_specs=VM,
        scratch_shapes=[
            pltpu.VMEM((2 * rows, channels), bf16),
            pltpu.VMEM((2 * rows, channels), bf16),
            pltpu.VMEM((marks, channels), bf16),
            pltpu.VMEM((marks, 2 * rows), bf16),
            pltpu.VMEM((marks, channels), bf16),
            pltpu.VMEM((slab, channels), f32),
            pltpu.VMEM((marks, channels), bf16),
            pltpu.VMEM((2, slab // 2, channels), bf16),
            pltpu.VMEM((3, slab, channels), bf16),
            pltpu.VMEM((slab, channels), bf16),
            pltpu.VMEM((RING * block, channels), bf16),
            pltpu.VMEM((RING, block, channels), bf16),
            pltpu.VMEM((2 * rows, channels), f32),
            pltpu.VMEM((rows, channels), f32),
            pltpu.SemaphoreType.DMA((copies,)),
            pltpu.SemaphoreType.DMA((copies,)),
        ],
        compiler_params=pltpu.CompilerParams(
            collective_id=1, has_side_effects=True, vmem_limit_bytes=44 << 20
        ),
        name="smooth",
    )(query, value, keys)


def finish_kernel(smooth, updated, w_out, result, term):
    wide = smooth[...]
    scaled = wide * lax.rsqrt(jnp.mean(wide * wide, axis=-1, keepdims=True) + 1e-6)
    term[...] = scaled
    result[...] = (updated[...].astype(f32) + dotf(scaled.astype(bf16), w_out[...])).astype(bf16)


def finish(smooth, updated, w_out):
    rows, channels = smooth.shape
    block = rows // 4
    tile = pl.BlockSpec((block, channels), lambda i: (i, 0))
    return pl.pallas_call(
        finish_kernel,
        out_shape=(
            jax.ShapeDtypeStruct((rows, channels), bf16),
            jax.ShapeDtypeStruct((rows, channels), f32),
        ),
        grid=(rows // block,),
        in_specs=[tile, tile, pl.BlockSpec((channels, channels), lambda i: (0, 0))],
        out_specs=(tile, tile),
        name="finish",
    )(smooth, updated, w_out)


def shards(
    groups, doms,
    nodes, neighbours, send_rows, landmark_ids,
    w_dst, w_src, w_msg, edge_bias, w_query, w_key, w_value, w_out,
):
    halo = halo_rows(groups, doms, nodes, send_rows)
    updated, query, value, keys = front(
        nodes, halo, neighbours, landmark_ids, w_dst, w_src, w_msg, edge_bias, w_query, w_key, w_value
    )
    smooth = smooth_rows(query, value, keys)
    return finish(smooth, updated, w_out)


def solution(mesh):
    groups, doms = mesh.shape["grp"], mesh.shape["dom"]
    split, line, whole = P(AXES, None), P(AXES), P()
    return jax.shard_map(
        functools.partial(shards, groups, doms),
        mesh=mesh,
        in_specs=(split, split, line, line) + (whole,) * 8,
        out_specs=(split, split),
        check_vma=False,
    )
```
